32 devices in a mesh: img: 8 (over z, y), pix: 4 (over x, core).
Axes of the slice: x: 2, y: 2, z: 4, core: 2. Of those that a mesh axis runs over, the one named last changes fastest.
Arguments:
- images: bfloat16 [3072, 16384], P('img', 'pix'), may hold values from -12 to 12
- inverse_noise_scale: float32 [3072], P('img'), may hold values from 0.4 to 4
- projections: bfloat16 [8192, 16384], P('img', 'pix'), may hold values from -1 to 1
- group_search_blocks: int32 [8, 16], P('img'), may hold values from 0 to 63, as said below
- search_list_count: int32 [8], P('img'), may hold values from 12 to 16, as said below
Outputs:
- projection_sums: float32 [8192, 16384], P('img', 'pix')
- log_evidence: float32 [3072], P(('img', 'pix'))
The draws below stay inside these ranges and needn't reach their ends.
Inputs may be any that keep to these rules, and one draw needn't show every extreme that they name: `group_search_blocks`: each row lists 16 different block ids; block b is owned by index b // 8 of img. Among the first search_list_count[g] entries of row g no owner appears more than 2 times, and in every draw one owner has 2 of its blocks among the first 2 entries of every row. `search_list_count`: some group's count is 16 in every draw.
All inputs are finite; a program needn't handle non-finite values.
Results may differ from the reference program's by a relative error of at most 0.004.
Values may be sent and summed in bfloat16 or wider, within the bound.
No kernel may reach another device: no remote copies, remote signals or barrier semaphores. Data moves between devices by JAX's collectives and lax.ppermute only.
A program may use at most 128 MiB of HBM per device.

```python
import math
import jax
import jax.numpy as jnp
from jax import lax

F = 16384
BLOCK = 128
BLK_DEV = 8
CAP = 2
MAXL = 16
GROUP_IMAGES = 384
NBLK = 64
NPROJ = 8192
NIMG = 3072
N_IMG = 8


def search_table(key):
    base = jax.random.fold_in(key, 11)
    key_hot, key_order, key_offset, key_count, key_long = jax.random.split(base, 5)
    hot_owner = jax.random.randint(key_hot, (), 0, N_IMG)
    owner_orders = jax.vmap(lambda single: jax.random.permutation(single, N_IMG - 1))(jax.random.split(key_order, N_IMG))
    order_table = jnp.concatenate([jnp.full((N_IMG, 1), hot_owner, jnp.int32), ((hot_owner + 1 + owner_orders) % N_IMG).astype(jnp.int32)], axis=1)
    offset_table = jax.vmap(lambda single: jax.random.permutation(single, BLK_DEV)[:CAP])(jax.random.split(key_offset, N_IMG * N_IMG))
    offset_table = offset_table.reshape(N_IMG, N_IMG, CAP)
    positions = jnp.arange(MAXL)
    which_owner = positions // CAP
    inner_slot = positions % CAP
    owners = order_table[:, which_owner]
    offsets = offset_table[jnp.arange(N_IMG)[:, None], which_owner[None, :], inner_slot[None, :]]
    table = (owners * BLK_DEV + offsets).astype(jnp.int32)
    counts = MAXL - 4 + jax.random.randint(key_count, (N_IMG,), 0, 5)
    longest = jax.random.randint(key_long, (), 0, N_IMG)
    counts = jnp.where(jnp.arange(N_IMG) == longest, MAXL, counts).astype(jnp.int32)
    return (table, counts)


def projection_field(key):
    base = jax.random.fold_in(key, 12)
    key_main = jax.random.fold_in(base, 0)
    field = jax.random.normal(key_main, (NPROJ, F), jnp.float32) * F ** (-0.5)
    return jnp.clip(field, -12.0 * F ** (-0.5), 12.0 * F ** (-0.5))


def draw_group_search_blocks(key, part):
    return search_table(key)[0]


def draw_search_list_count(key, part):
    return search_table(key)[1]


def draw_projections(key, part):
    return projection_field(key).astype(jnp.bfloat16)


def draw_images(key, part):
    base = jax.random.fold_in(key, 13)
    key_main = jax.random.fold_in(base, 0)
    result = jax.random.normal(key_main, (NIMG, F), jnp.float32)
    return jnp.clip(result, -12.0, 12.0).astype(jnp.bfloat16)


def block_scale(key, extent, pieces, smallest, high):
    factor_of, own = 1.0, jax.random.fold_in(key, 6)
    for dim, parts in pieces:
        heights = jnp.exp(jax.random.uniform(jax.random.fold_in(own, dim), (parts,), jnp.float32, smallest / len(pieces), high / len(pieces)))
        factor_of = factor_of * jnp.repeat(heights, extent[dim] // parts).reshape([-1 if axis == dim else 1 for axis in range(len(extent))])
    return factor_of


def setup_inputs(seed: int = 0) -> dict:
    key_list = jax.random.split(jax.random.key(seed), 6)
    return {
        "images": draw_images(jax.random.fold_in(key_list[5], 71), 0),
        "inverse_noise_scale": jnp.clip(jnp.exp(math.log(4.0) - 2.3025851 * jax.random.uniform(key_list[1], (NIMG,), jnp.float32) ** block_scale(key_list[1], (NIMG,), ((0, 8),), -0.2, 0.2)), 0.4, 4.0),
        "projections": draw_projections(jax.random.fold_in(key_list[5], 71), 0),
        "group_search_blocks": draw_group_search_blocks(jax.random.fold_in(key_list[5], 71), 0),
        "search_list_count": draw_search_list_count(jax.random.fold_in(key_list[5], 71), 0),
    }


def reference(images, inverse_noise_scale, projections, group_search_blocks, search_list_count):
    blocks = projections.reshape(NBLK, BLOCK, F)
    images_by_group = images.reshape(N_IMG, GROUP_IMAGES, F)
    noise_scale_factors = inverse_noise_scale.reshape(N_IMG, GROUP_IMAGES)
    positions = jnp.arange(MAXL, dtype=jnp.int32)

    def visit_block(running_total, inputs):
        members, scaling, chosen, listed = inputs
        live_entry = positions < listed
        fetched = jnp.take(blocks, chosen.astype(jnp.int32), axis=0).astype(jnp.float32)
        pixels = members.astype(jnp.float32)
        scores = jnp.einsum("kbf,if->ikb", fetched, pixels, precision=lax.Precision.HIGHEST)
        scores = scores * scaling[:, None, None]
        live_mask = live_entry[None, :, None]
        scores = jnp.where(live_mask, scores, jnp.float32(-1e30))
        row_peak = jnp.max(scores, axis=(1, 2), keepdims=True)
        exponent = jnp.where(live_mask, jnp.exp(scores - row_peak), jnp.float32(0.0))
        row_total = jnp.sum(exponent, axis=(1, 2), keepdims=True)
        weights = (exponent / row_total).astype(jnp.bfloat16)
        block_sums = jnp.einsum("ikb,if->kbf", weights.astype(jnp.float32), pixels, precision=lax.Precision.HIGHEST)
        block_sums = block_sums.astype(jnp.bfloat16)
        running_total = running_total.at[chosen.astype(jnp.int32)].add(block_sums.astype(jnp.float32))
        return running_total, (row_peak + jnp.log(row_total)).reshape(-1)

    initial_partial_sums = jnp.zeros((NBLK, BLOCK, F), jnp.float32)
    running_total, marginal_likelihood = lax.scan(visit_block, initial_partial_sums, (images_by_group, noise_scale_factors, group_search_blocks, search_list_count))
    return running_total.reshape(NPROJ, F), marginal_likelihood.reshape(-1)
```

```python
import jax
import jax.numpy as jnp
from jax import lax
from jax.experimental import pallas as pl
from jax.experimental.pallas import tpu as pltpu
from jax.sharding import PartitionSpec as P

BLOCK = 128
CAP = 2
MAXL = 16
WIDE = CAP * BLOCK
CORES = 2
CHUNK_PARTS = (2, 2, 2)


def ring_order(n):
    rows = 4 if n % 4 == 0 and n >= 8 else 1
    cols = n // rows
    if rows == 1 or cols == 1:
        return list(range(n))
    walk = []
    for row in range(rows):
        across = range(1, cols) if row % 2 == 0 else range(cols - 1, 0, -1)
        walk += [row * cols + col for col in across]
    return walk + [row * cols for row in range(rows - 1, -1, -1)]


def score_body(n_pieces, ids_ref, offs_ref, *refs):
    piece_refs = refs[:n_pieces]
    proj_ref, out_ref = refs[n_pieces], refs[-1]
    for k in range(n_pieces):

        @pl.when(pl.program_id(0) == k)
        def _(k=k):
            out_ref[0] = lax.dot_general(
                piece_refs[k][...],
                proj_ref[...],
                (((1,), (1,)), ((), ())),
                preferred_element_type=jnp.float32,
            )


def score_pieces(pieces, halves, group_ids, offsets, projections, n_groups, rows, before):
    count = len(pieces)
    pixels = projections.shape[1]
    height = pieces[0].shape[0]
    in_specs = [pl.BlockSpec((height, pixels), lambda k, j, ids, offs: (0, 0)) for _ in pieces]
    in_specs.append(pl.BlockSpec((BLOCK, pixels), lambda k, j, ids, offs: (offs[k * CAP + j], 0)))
    operands = [*pieces, projections]
    aliases = {}
    if before is not None:
        in_specs.append(pl.BlockSpec(memory_space=pl.ANY))
        operands.append(before)
        aliases = {2 + len(operands) - 1: 0}
    if halves:
        out_map = lambda k, j, ids, offs: (ids[k], k, j)
    else:
        out_map = lambda k, j, ids, offs: (ids[k], 0, j)
    return pl.pallas_call(
        lambda *refs: score_body(count, *refs),
        out_shape=jax.ShapeDtypeStruct((n_groups, rows, WIDE), jnp.float32),
        grid_spec=pltpu.PrefetchScalarGridSpec(
            num_scalar_prefetch=2,
            grid=(count, CAP),
            in_specs=in_specs,
            out_specs=pl.BlockSpec((1, height, BLOCK), out_map),
        ),
        input_output_aliases=aliases,
        compiler_params=pltpu.CompilerParams(
            dimension_semantics=("arbitrary", "arbitrary"), vmem_limit_bytes=24 << 20
        ),
        cost_estimate=pl.CostEstimate(
            flops=2 * count * height * WIDE * pixels,
            bytes_accessed=count * (height + WIDE) * pixels * 2 + count * height * WIDE * 4,
            transcendentals=0,
        ),
        name="scores",
    )(group_ids, offsets, *operands)


def softmax_body(used_ref, total_ref, scale_ref, weight_ref, evidence_ref):
    n = total_ref.shape[0]
    scale = scale_ref[...]
    peak = jnp.full(scale.shape, -jnp.inf, jnp.float32)

    def logits(o, j):
        value = total_ref[o, :, j * BLOCK : (j + 1) * BLOCK] * scale
        live = used_ref[o * CAP + j] > 0
        return jnp.where(live, value, jnp.float32(-1e30)), live

    for o in range(n):
        for j in range(CAP):
            peak = jnp.maximum(peak, jnp.max(logits(o, j)[0], axis=1, keepdims=True))
    total = jnp.zeros(scale.shape, jnp.float32)
    for o in range(n):
        for j in range(CAP):
            value, live = logits(o, j)
            raised = jnp.where(live, jnp.exp(value - peak), jnp.float32(0.0))
            total_ref[o, :, j * BLOCK : (j + 1) * BLOCK] = raised
            total = total + jnp.sum(raised, axis=1, keepdims=True)
    for o in range(n):
        weight_ref[o] = (total_ref[o] / total).astype(jnp.bfloat16)
    evidence_ref[...] = peak + jnp.log(total)


def softmax(totals, scale, used):
    n, share, _ = totals.shape

    def body(used_ref, total_in, scale_ref, weight_ref, evidence_ref, work):
        work[...] = total_in[...]
        softmax_body(used_ref, work, scale_ref, weight_ref, evidence_ref)

    return pl.pallas_call(
        body,
        out_shape=(
            jax.ShapeDtypeStruct((n, share, WIDE), jnp.bfloat16),
            jax.ShapeDtypeStruct((share, 1), jnp.float32),
        ),
        in_specs=[
            pl.BlockSpec(memory_space=pltpu.SMEM),
            pl.BlockSpec(memory_space=pltpu.VMEM),
            pl.BlockSpec(memory_space=pltpu.VMEM),
        ],
        out_specs=(
            pl.BlockSpec(memory_space=pltpu.VMEM),
            pl.BlockSpec(memory_space=pltpu.VMEM),
        ),
        scratch_shapes=[pltpu.VMEM((n, share, WIDE), jnp.float32)],
        compiler_params=pltpu.CompilerParams(vmem_limit_bytes=16 << 20),
        cost_estimate=pl.CostEstimate(
            flops=6 * n * share * WIDE,
            bytes_accessed=6 * n * share * WIDE,
            transcendentals=n * share * WIDE,
        ),
        name="softmax",
    )(used, totals, scale)


def sums_kernel(images_of, weights_of, group_ids, offsets, share_index, owned_rows, pixels, n):
    tile = 512 if pixels % 512 == 0 else pixels
    flat_images, place = [], []
    for r, entries in enumerate(images_of):
        place.append([])
        for array in entries:
            place[r].append(len(flat_images))
            flat_images.append(array)
    flat_weights = [array for entries in weights_of for array in entries]
    n_images, n_weights = len(flat_images), len(flat_weights)
    shares = [entries[0].shape[1] for entries in weights_of]
    per_chunk = len(weights_of[0])
    depth = sum(share * per_chunk for share in shares)

    def body(ids_ref, offs_ref, share_ref, *refs):
        image_refs = refs[:n_images]
        weight_refs = refs[n_images : n_images + n_weights]
        out_ref, rows_ref, cols_ref = refs[n_images + n_weights :]

        @pl.when(pl.program_id(0) == 0)
        def _():
            base = 0
            for c, share in enumerate(shares):
                for k in range(per_chunk):
                    first = pl.multiple_of(base + share_ref[k] * share, share)
                    rows_ref[:, pl.ds(first, share), :] = weight_refs[c * per_chunk + k][...]
                base += share * per_chunk
            for g in range(n):
                cols_ref[g] = rows_ref[g].T

        out_ref[...] = jnp.zeros_like(out_ref)
        for r in range(n):
            g = ids_ref[r]
            pixels_of = jnp.concatenate([image_refs[i][...] for i in place[r]], axis=0)
            sums = jnp.dot(cols_ref[g], pixels_of, preferred_element_type=jnp.float32)
            sums = sums.astype(jnp.bfloat16).astype(jnp.float32)
            for j in range(CAP):
                at = pl.ds(pl.multiple_of(offs_ref[g * CAP + j] * BLOCK, BLOCK), BLOCK)
                out_ref[at, :] += sums[j * BLOCK : (j + 1) * BLOCK]

    return pl.pallas_call(
        body,
        out_shape=jax.ShapeDtypeStruct((owned_rows, pixels), jnp.float32),
        grid_spec=pltpu.PrefetchScalarGridSpec(
            num_scalar_prefetch=3,
            grid=(pixels // tile,),
            in_specs=[
                pl.BlockSpec((array.shape[0], tile), lambda t, ids, offs, sh: (0, t))
                for array in flat_images
            ]
            + [
                pl.BlockSpec(array.shape, lambda t, ids, offs, sh: (0, 0, 0))
                for array in flat_weights
            ],
            out_specs=pl.BlockSpec((owned_rows, tile), lambda t, ids, offs, sh: (0, t)),
            scratch_shapes=[
                pltpu.VMEM((n, depth, WIDE), jnp.bfloat16),
                pltpu.VMEM((n, WIDE, depth), jnp.bfloat16),
            ],
        ),
        compiler_params=pltpu.CompilerParams(
            dimension_semantics=("arbitrary",), vmem_limit_bytes=48 << 20
        ),
        cost_estimate=pl.CostEstimate(
            flops=2 * n * depth * WIDE * pixels,
            bytes_accessed=n * depth * (pixels + WIDE) * 2 + owned_rows * pixels * 4,
            transcendentals=0,
        ),
        name="sums",
    )(group_ids, offsets, share_index, *flat_images, *flat_weights)


def on_device(images, inverse_noise_scale, projections, group_search_blocks, search_list_count):
    group_rows, pixels = images.shape
    n = lax.axis_size("img")
    n_pix = lax.axis_size("pix")
    n_x = n_pix // CORES
    owned = projections.shape[0] // BLOCK
    me = lax.axis_index("img")
    pix = lax.axis_index("pix")
    my_x, my_core = pix // CORES, pix % CORES
    share_rows = group_rows // n_pix

    ring = ring_order(n)
    right = [(ring[k], ring[(k + 1) % n]) for k in range(n)]
    left = [(b, a) for a, b in right]
    ring_ids = jnp.array(ring, jnp.int32)
    pos_table = [0] * n
    for k, index in enumerate(ring):
        pos_table[index] = k
    ring_pos = jnp.array(pos_table, jnp.int32)
    my_pos = ring_pos[me]
    shifts = [0]
    for s in range(1, n // 2):
        shifts += [-s, s]
    shifts.append(n // 2)
    group_ids = ring_ids[(my_pos + jnp.array(shifts, jnp.int32)) % n]

    unit = share_rows // sum(CHUNK_PARTS)
    shares = [unit * part for part in CHUNK_PARTS]
    by_share = images.reshape(n_pix, share_rows, pixels)
    scale_mine = lax.dynamic_slice_in_dim(inverse_noise_scale, pix * share_rows, share_rows)

    note = jnp.concatenate(
        [group_search_blocks[0], search_list_count, jnp.zeros((2 * MAXL - MAXL - 1,), jnp.int32)]
    )
    notes = lax.all_to_all(jnp.broadcast_to(note, (n, 2 * MAXL)), "img", 0, 0, tiled=True)
    lists, counts = notes[:, :MAXL], notes[:, MAXL]
    positions = jnp.arange(MAXL, dtype=jnp.int32)
    slots = jnp.arange(CAP, dtype=jnp.int32)
    hit = (positions[None, :] < counts[:, None]) & (lists // owned == me)
    earlier = positions[None, :] < positions[:, None]
    rank = jnp.sum((hit[:, None, :] & earlier[None]).astype(jnp.int32), axis=2)
    pick = hit[:, None, :] & (rank[:, None, :] == slots[None, :, None])
    slot_offset = jnp.sum(jnp.where(pick, (lists % owned)[:, None, :], 0), axis=2)
    flat_offset = slot_offset.reshape(-1)
    piece_offset = slot_offset[group_ids].reshape(-1)

    own_live = positions < search_list_count[0]
    own_owner = group_search_blocks[0] // owned
    per_owner = jnp.sum(
        (own_live[None, :] & (own_owner[None, :] == jnp.arange(n, dtype=jnp.int32)[:, None])).astype(
            jnp.int32
        ),
        axis=1,
    )
    used = (slots[None, :] < per_owner[:, None]).astype(jnp.int32).reshape(-1)

    core_swap = [(p, p ^ 1) for p in range(n_pix)]

    def x_shift(k):
        return [
            (x * CORES + core, ((x + k) % n_x) * CORES + core)
            for x in range(n_x)
            for core in range(CORES)
        ]

    images_of = [[] for _ in range(n)]
    weights_of, evidence = [], []
    start, gate = 0, None
    for share in shares:
        rows = share * n_pix
        chunk = by_share[:, start : start + share].reshape(rows, pixels)
        if gate is not None:
            chunk, _ = lax.optimization_barrier((chunk, gate))
        pieces = [chunk]
        from_left = from_right = chunk
        half = rows // 2
        for s in range(1, n // 2):
            from_left = lax.ppermute(from_left, "img", right)
            from_right = lax.ppermute(from_right, "img", left)
            pieces += [from_left, from_right]
            if s == 2:
                gate = (from_left[:16, :BLOCK], from_right[:16, :BLOCK])
        far = [
            lax.ppermute(from_left[:half], "img", right),
            lax.ppermute(from_right[half:], "img", left),
        ]
        for r in range(n - 1):
            images_of[r].append(pieces[r])
        images_of[n - 1] += far

        def scored(first, count, group, before, halves=False):
            ids = group_ids[first : first + 1] if halves else group_ids[first : first + count]
            offs = piece_offset[first * CAP : (first + (1 if halves else count)) * CAP]
            if halves:
                ids, offs = jnp.tile(ids, 2), jnp.tile(offs, 2)
            return score_pieces(group, halves, ids, offs, projections, n, rows, before)

        scores = scored(0, 1, pieces[:1], None)
        for s in range(1, n // 2):
            scores = scored(2 * s - 1, 2, pieces[2 * s - 1 : 2 * s + 1], scores)
        scores = scored(n - 1, 1, far, scores, True)

        scores = scores.reshape(n, n_x, CORES, share, WIDE)
        give = lax.dynamic_index_in_dim(scores, 1 - my_core, 2, keepdims=False)
        keep = lax.dynamic_index_in_dim(scores, my_core, 2, keepdims=False)
        half_sum = keep + lax.ppermute(give, "pix", core_swap)
        total = lax.dynamic_index_in_dim(half_sum, my_x, 1, keepdims=False)
        arrivals = [
            lax.ppermute(
                lax.dynamic_index_in_dim(half_sum, (my_x + k) % n_x, 1, keepdims=False),
                "pix",
                x_shift(k),
            )
            for k in range(1, n_x)
        ]
        for arrival in arrivals:
            total = total + arrival
        home = lax.all_to_all(total, "img", 0, 0, tiled=True)
        scale = lax.slice_in_dim(scale_mine, start, start + share).reshape(share, 1)
        weights, marginal = softmax(home, scale, used)
        evidence.append(marginal.reshape(share))
        back = lax.all_to_all(weights, "img", 0, 0, tiled=True)
        same_core = [back] + [lax.ppermute(back, "pix", x_shift(k)) for k in range(1, n_x)]
        other_core = [lax.ppermute(array, "pix", core_swap) for array in same_core]
        weights_of.append(same_core + other_core)
        start += share

    steps = jnp.arange(n_x, dtype=jnp.int32)
    from_x = (my_x - steps) % n_x
    share_index = jnp.concatenate([from_x * CORES + my_core, from_x * CORES + (1 - my_core)])
    sums = sums_kernel(
        images_of,
        weights_of,
        group_ids,
        flat_offset,
        share_index.astype(jnp.int32),
        owned * BLOCK,
        pixels,
        n,
    )
    return sums, jnp.concatenate(evidence)


def solution(mesh):
    placed = (P("img", "pix"), P("img"), P("img", "pix"), P("img", None), P("img"))
    return jax.shard_map(
        on_device,
        mesh=mesh,
        in_specs=placed,
        out_specs=(P("img", "pix"), P(("img", "pix"))),
        check_vma=False,
    )
```

```python
import jax
import jax.numpy as jnp
from jax import lax
from jax.experimental import pallas as pl
from jax.experimental.pallas import tpu as pltpu
from jax.sharding import PartitionSpec as P

BLOCK = 128
CAP = 2
MAXL = 16
WIDE = CAP * BLOCK
CORES = 2
CHUNK_PARTS = (2, 2, 2)
SCORE_VMEM = 24 << 20


def ring_order(n):
    rows = 4 if n % 4 == 0 and n >= 8 else 1
    cols = n // rows
    if rows == 1 or cols == 1:
        return list(range(n))
    walk = []
    for row in range(rows):
        across = range(1, cols) if row % 2 == 0 else range(cols - 1, 0, -1)
        walk += [row * cols + col for col in across]
    return walk + [row * cols for row in range(rows - 1, -1, -1)]


def score_pieces(pieces, merged, group_ids, offsets, projections, before, shape):
    count = 1 if merged else len(pieces)
    pixels = projections.shape[1]
    height = shape[1]

    def body(ids_ref, offs_ref, *refs):
        piece_refs = refs[: len(pieces)]
        proj_ref, out_ref = refs[len(pieces)], refs[-1]

        def score(rows):
            out_ref[0] = lax.dot_general(
                rows, proj_ref[...], (((1,), (1,)), ((), ())), preferred_element_type=jnp.float32
            )

        if count == 1:
            score(jnp.concatenate([ref[...] for ref in piece_refs], axis=0))
            return
        for k in range(count):

            @pl.when(pl.program_id(0) == k)
            def _(k=k):
                score(piece_refs[k][...])

    in_specs = [pl.BlockSpec(p.shape, lambda k, j, ids, offs: (0, 0)) for p in pieces]
    in_specs.append(pl.BlockSpec((BLOCK, pixels), lambda k, j, ids, offs: (offs[k * CAP + j], 0)))
    operands = [*pieces, projections]
    aliases = {}
    if before is not None:
        in_specs.append(pl.BlockSpec(memory_space=pl.ANY))
        operands.append(before)
        aliases = {2 + len(operands) - 1: 0}
    return pl.pallas_call(
        body,
        out_shape=jax.ShapeDtypeStruct(shape, jnp.float32),
        grid_spec=pltpu.PrefetchScalarGridSpec(
            num_scalar_prefetch=2,
            grid=(count, CAP),
            in_specs=in_specs,
            out_specs=pl.BlockSpec((1, height, BLOCK), lambda k, j, ids, offs: (ids[k], 0, j)),
        ),
        input_output_aliases=aliases,
        compiler_params=pltpu.CompilerParams(
            dimension_semantics=("arbitrary", "arbitrary"), vmem_limit_bytes=SCORE_VMEM
        ),
        cost_estimate=pl.CostEstimate(
            flops=2 * count * height * WIDE * pixels,
            bytes_accessed=count * (height + WIDE) * pixels * 2 + count * height * WIDE * 4,
            transcendentals=0,
        ),
        name="scores",
    )(group_ids, offsets, *operands)


def softmax_body(used_ref, total_ref, scale_ref, weight_ref, evidence_ref):
    n = total_ref.shape[0]
    scale = scale_ref[...]
    peak = jnp.full(scale.shape, -jnp.inf, jnp.float32)

    def logits(o, j):
        value = total_ref[o, :, j * BLOCK : (j + 1) * BLOCK] * scale
        live = used_ref[o * CAP + j] > 0
        return jnp.where(live, value, jnp.float32(-1e30)), live

    for o in range(n):
        for j in range(CAP):
            peak = jnp.maximum(peak, jnp.max(logits(o, j)[0], axis=1, keepdims=True))
    total = jnp.zeros(scale.shape, jnp.float32)
    for o in range(n):
        for j in range(CAP):
            value, live = logits(o, j)
            raised = jnp.where(live, jnp.exp(value - peak), jnp.float32(0.0))
            total_ref[o, :, j * BLOCK : (j + 1) * BLOCK] = raised
            total = total + jnp.sum(raised, axis=1, keepdims=True)
    for o in range(n):
        weight_ref[o] = (total_ref[o] / total).astype(jnp.bfloat16)
    marginal = jnp.broadcast_to(peak + jnp.log(total), (total.shape[0], BLOCK))
    evidence_ref[...] = marginal.T[:1]


def softmax(totals, scale, used):
    n, share, _ = totals.shape

    def body(used_ref, total_in, scale_ref, weight_ref, evidence_ref, work):
        work[...] = total_in[...]
        softmax_body(used_ref, work, scale_ref, weight_ref, evidence_ref)

    return pl.pallas_call(
        body,
        out_shape=(
            jax.ShapeDtypeStruct((n, share, WIDE), jnp.bfloat16),
            jax.ShapeDtypeStruct((1, share), jnp.float32),
        ),
        in_specs=[
            pl.BlockSpec(memory_space=pltpu.SMEM),
            pl.BlockSpec(memory_space=pltpu.VMEM),
            pl.BlockSpec(memory_space=pltpu.VMEM),
        ],
        out_specs=(
            pl.BlockSpec(memory_space=pltpu.VMEM),
            pl.BlockSpec(memory_space=pltpu.VMEM),
        ),
        scratch_shapes=[pltpu.VMEM((n, share, WIDE), jnp.float32)],
        compiler_params=pltpu.CompilerParams(vmem_limit_bytes=16 << 20),
        cost_estimate=pl.CostEstimate(
            flops=6 * n * share * WIDE,
            bytes_accessed=6 * n * share * WIDE,
            transcendentals=n * share * WIDE,
        ),
        name="softmax",
    )(used, totals, scale)


def sums_kernel(images_of, weights, group_ids, offsets, owned_rows, pixels, n):
    tile = 512 if pixels % 512 == 0 else pixels
    flat_images, place = [], []
    for r, entries in enumerate(images_of):
        place.append([])
        for array in entries:
            place[r].append(len(flat_images))
            flat_images.append(array)
    n_images, n_weights = len(flat_images), len(weights)
    depth = sum(array.shape[1] for array in weights)

    def body(ids_ref, offs_ref, *refs):
        image_refs = refs[:n_images]
        weight_refs = refs[n_images : n_images + n_weights]
        out_ref, rows_ref, cols_ref = refs[n_images + n_weights :]

        @pl.when(pl.program_id(0) == 0)
        def _():
            first = 0
            for ref in weight_refs:
                rows_ref[:, first : first + ref.shape[1], :] = ref[...]
                first += ref.shape[1]
            for g in range(n):
                cols_ref[g] = rows_ref[g].T

        out_ref[...] = jnp.zeros_like(out_ref)
        for r in range(n):
            g = ids_ref[r]
            rows = jnp.concatenate([image_refs[i][...] for i in place[r]], axis=0)
            sums = jnp.dot(cols_ref[g], rows, preferred_element_type=jnp.float32)
            sums = sums.astype(jnp.bfloat16).astype(jnp.float32)
            for j in range(CAP):
                at = pl.ds(pl.multiple_of(offs_ref[g * CAP + j] * BLOCK, BLOCK), BLOCK)
                out_ref[at, :] += sums[j * BLOCK : (j + 1) * BLOCK]

    return pl.pallas_call(
        body,
        out_shape=jax.ShapeDtypeStruct((owned_rows, pixels), jnp.float32),
        grid_spec=pltpu.PrefetchScalarGridSpec(
            num_scalar_prefetch=2,
            grid=(pixels // tile,),
            in_specs=[
                pl.BlockSpec((array.shape[0], tile), lambda t, ids, offs: (0, t))
                for array in flat_images
            ]
            + [pl.BlockSpec(array.shape, lambda t, ids, offs: (0, 0, 0)) for array in weights],
            out_specs=pl.BlockSpec((owned_rows, tile), lambda t, ids, offs: (0, t)),
            scratch_shapes=[
                pltpu.VMEM((n, depth, WIDE), jnp.bfloat16),
                pltpu.VMEM((n, WIDE, depth), jnp.bfloat16),
            ],
        ),
        compiler_params=pltpu.CompilerParams(
            dimension_semantics=("arbitrary",), vmem_limit_bytes=48 << 20
        ),
        cost_estimate=pl.CostEstimate(
            flops=2 * n * depth * WIDE * pixels,
            bytes_accessed=n * depth * (pixels + WIDE) * 2 + owned_rows * pixels * 4,
            transcendentals=0,
        ),
        name="sums",
    )(group_ids, offsets, *flat_images, *weights)


def on_device(images, inverse_noise_scale, projections, group_search_blocks, search_list_count):
    group_rows, pixels = images.shape
    n = lax.axis_size("img")
    n_pix = lax.axis_size("pix")
    n_x = n_pix // CORES
    owned = projections.shape[0] // BLOCK
    me = lax.axis_index("img")
    pix = lax.axis_index("pix")
    my_x, my_core = pix // CORES, pix % CORES
    share_rows = group_rows // n_pix

    ring = ring_order(n)
    to_right = [(ring[k], ring[(k + 1) % n]) for k in range(n)]
    to_left = [(b, a) for a, b in to_right]
    ring_ids = jnp.array(ring, jnp.int32)
    pos_table = [0] * n
    for k, index in enumerate(ring):
        pos_table[index] = k
    ring_pos = jnp.array(pos_table, jnp.int32)
    my_pos = ring_pos[me]
    shifts = [0]
    for s in range(1, n // 2):
        shifts += [-s, s]
    shifts.append(n // 2)
    group_ids = ring_ids[(my_pos + jnp.array(shifts, jnp.int32)) % n]

    scale_mine = lax.dynamic_slice_in_dim(inverse_noise_scale, pix * share_rows, share_rows)

    note = jnp.concatenate(
        [group_search_blocks[0], search_list_count, jnp.zeros((2 * MAXL - MAXL - 1,), jnp.int32)]
    )
    notes = lax.all_to_all(jnp.broadcast_to(note, (n, 2 * MAXL)), "img", 0, 0, tiled=True)
    lists, counts = notes[:, :MAXL], notes[:, MAXL]
    positions = jnp.arange(MAXL, dtype=jnp.int32)
    slots = jnp.arange(CAP, dtype=jnp.int32)
    hit = (positions[None, :] < counts[:, None]) & (lists // owned == me)
    earlier = positions[None, :] < positions[:, None]
    rank = jnp.sum((hit[:, None, :] & earlier[None]).astype(jnp.int32), axis=2)
    pick = hit[:, None, :] & (rank[:, None, :] == slots[None, :, None])
    slot_offset = jnp.sum(jnp.where(pick, (lists % owned)[:, None, :], 0), axis=2)
    flat_offset = slot_offset.reshape(-1)
    piece_offset = slot_offset[group_ids].reshape(-1)

    own_live = positions < search_list_count[0]
    own_owner = group_search_blocks[0] // owned
    per_owner = jnp.sum(
        (own_live[None, :] & (own_owner[None, :] == jnp.arange(n, dtype=jnp.int32)[:, None])).astype(
            jnp.int32
        ),
        axis=1,
    )
    used = (slots[None, :] < per_owner[:, None]).astype(jnp.int32).reshape(-1)

    core_swap = [(p, p ^ 1) for p in range(n_pix)]

    def x_shift(k):
        return [
            (x * CORES + core, ((x + k) % n_x) * CORES + core)
            for x in range(n_x)
            for core in range(CORES)
        ]

    unit = share_rows // sum(CHUNK_PARTS)
    shares = [unit * part for part in CHUNK_PARTS]
    starts = [sum(shares[:c]) for c in range(len(shares))]
    far_step = n // 2

    def packet(c, a):
        rows = []
        for b in range(n_x):
            q = ((my_x + b) % n_x) * CORES + (my_core ^ a)
            rows.append(
                lax.dynamic_slice_in_dim(images, q * share_rows + starts[c], shares[c], axis=0)
            )
        return jnp.concatenate(rows, axis=0)

    messages = [
        (c, a, s) for c in range(len(shares)) for s in range(1, far_step + 1) for a in (1, 0)
    ]
    pieces = {(c, a): {} for c in range(len(shares)) for a in (0, 1)}
    scores, score_tick = {}, {}

    def score(c, a, places):
        rows = shares[c] * n_x
        group = [array for r in places for array in pieces[c, a][r]]
        ids = jnp.stack([group_ids[r] for r in places])
        offs = jnp.concatenate([piece_offset[r * CAP : (r + 1) * CAP] for r in places])
        scores[c, a] = score_pieces(
            group, places == [n - 1], ids, offs, projections, scores.get((c, a)), (n, rows, WIDE)
        )

    weights_of, evidence = {}, {}

    def finish(c):
        share = shares[c]
        (got,) = yield [lax.ppermute(scores[c, 1], "pix", core_swap)], 1
        whole = (scores[c, 0] + got).reshape(n, n_x, share, WIDE)
        parts = [whole[:, 0]] + [
            lax.ppermute(whole[:, b], "pix", x_shift(b)) for b in range(1, n_x)
        ]
        parts = yield parts, 1
        total = parts[0]
        for part in parts[1:]:
            total = total + part
        (home,) = yield [lax.all_to_all(total, "img", 0, 0, tiled=True)], 2
        scale = lax.slice_in_dim(scale_mine, starts[c], starts[c] + share).reshape(share, 1)
        weights, marginal = softmax(home, scale, used)
        evidence[c] = marginal.reshape(share)
        (back,) = yield [lax.all_to_all(weights, "img", 0, 0, tiled=True)], 2
        same = yield [back] + [lax.ppermute(back, "pix", x_shift(-b)) for b in range(1, n_x)], 1
        other = yield [lax.ppermute(array, "pix", core_swap) for array in same], 1
        weights_of[c] = [*same, *other]

    arrived = {}
    due = {}
    running = {}

    def advance(c, sent):
        try:
            values, lag = running[c].send(sent)
            due.setdefault(tick + lag, []).append((c, list(values)))
        except StopIteration:
            pass

    tick = 0
    while tick < len(messages) + 2 or any(t >= tick for t in due):
        flying = tick < len(messages)
        ring = []
        if tick >= 2 and tick - 2 in arrived:
            ring += list(arrived[tick - 2])
        n_arrived = len(ring)
        fresh = flying and messages[tick][2] == 1
        if fresh:
            ring.append(packet(*messages[tick][:2]))
        waiting = due.pop(tick, [])
        scored = [key for key in scores if score_tick.get(key) == tick] if tick else []
        bundle = ring + [scores[key] for key in scored] + [v for _, vs in waiting for v in vs]
        if tick >= 2 and len(bundle) > 1:
            bundle = list(lax.optimization_barrier(tuple(bundle)))
        ring, rest = bundle[: len(ring)], bundle[len(ring) :]
        for key in scored:
            scores[key] = rest.pop(0)
        if n_arrived:
            arrived[tick - 2] = ring[:2]
            c, a, s = messages[tick - 2]
            if s == far_step:
                pieces[c, a][n - 1] = ring[:2]
            else:
                pieces[c, a][2 * s - 1], pieces[c, a][2 * s] = [ring[0]], [ring[1]]
        if flying:
            c, a, s = messages[tick]
            if fresh:
                pieces[c, a][0] = [ring[-1]]
                left = right = ring[-1]
            else:
                left, right = pieces[c, a][2 * s - 3][0], pieces[c, a][2 * s - 2][0]
            if s == far_step:
                middle = left.shape[0] // 2
                left, right = left[:middle], right[middle:]
            arrived[tick] = (
                lax.ppermute(left, "img", to_right),
                lax.ppermute(right, "img", to_left),
            )
            if fresh:
                score(c, a, [0])
                score_tick[c, a] = tick + 1
        if n_arrived:
            c, a, s = messages[tick - 2]
            score(c, a, [n - 1] if s == far_step else [2 * s - 1, 2 * s])
            score_tick[c, a] = tick + 1
        for c, values in waiting:
            sent, rest = rest[: len(values)], rest[len(values) :]
            advance(c, sent)
        for c in range(len(shares)):
            if c not in running and messages.index((c, 1, far_step)) + 3 == tick:
                running[c] = finish(c)
                advance(c, None)
        tick += 1

    images_of = [
        [array for c in range(len(shares)) for a in (0, 1) for array in pieces[c, a][r]]
        for r in range(n)
    ]
    weights = [array for c in range(len(shares)) for array in weights_of[c]]
    sums = sums_kernel(images_of, weights, group_ids, flat_offset, owned * BLOCK, pixels, n)
    return sums, jnp.concatenate([evidence[c] for c in range(len(shares))])


def solution(mesh):
    placed = (P("img", "pix"), P("img"), P("img", "pix"), P("img", None), P("img"))
    return jax.shard_map(
        on_device,
        mesh=mesh,
        in_specs=placed,
        out_specs=(P("img", "pix"), P(("img", "pix"))),
        check_vma=False,
    )
```

```python
import jax
import jax.numpy as jnp
from jax import lax
from jax.experimental import pallas as pl
from jax.experimental.pallas import tpu as pltpu
from jax.sharding import PartitionSpec as P

BLOCK = 128
CAP = 2
MAXL = 16
WIDE = CAP * BLOCK
CORES = 2
CHUNK_PARTS = (2, 1)
SCORE_VMEM = 56 << 20
SUMS_VMEM = 28 << 20
LIST_TICK = 5


def ring_order(n):
    rows = 4 if n % 4 == 0 and n >= 8 else 1
    cols = n // rows
    if rows == 1 or cols == 1:
        return list(range(n))
    walk = []
    for row in range(rows):
        across = range(1, cols) if row % 2 == 0 else range(cols - 1, 0, -1)
        walk += [row * cols + col for col in across]
    return walk + [row * cols for row in range(rows - 1, -1, -1)]


def in_hbm(array):
    return pltpu.with_memory_space_constraint(array, pltpu.HBM)


def score_pieces(pieces, group_ids, offsets, projections, before, shape):
    count = len(pieces)
    pixels = projections.shape[1]
    tile = 512 if pixels % 512 == 0 else pixels
    rows = shape[1]
    flat = [array for piece in pieces for array in piece]
    place = [[i for i, array in enumerate(flat) if any(array is a for a in p)] for p in pieces]
    n_flat, n_blocks = len(flat), count * CAP

    def body(ids_ref, offs_ref, *refs):
        row_refs, block_refs, out_ref = refs[:n_flat], refs[n_flat : n_flat + n_blocks], refs[-2]
        acc_ref = refs[-1]
        step, last = pl.program_id(0), pl.num_programs(0) - 1

        @pl.when(step == 0)
        def _():
            acc_ref[...] = jnp.zeros_like(acc_ref)

        for k in range(count):
            left = jnp.concatenate([row_refs[i][...] for i in place[k]], axis=0)
            right = jnp.concatenate([block_refs[k * CAP + j][...] for j in range(CAP)], axis=0)
            acc_ref[k] += lax.dot_general(
                left, right, (((1,), (1,)), ((), ())), preferred_element_type=jnp.float32
            )

        if count == 1:

            @pl.when(step == last)
            def _():
                out_ref[...] = acc_ref[...]

        else:

            @pl.when(step == last)
            def _():
                for k in range(count):
                    out_ref[ids_ref[k]] = acc_ref[k]

    def block_spec(m):
        return pl.BlockSpec((BLOCK, tile), lambda t, ids, offs: (offs[m], t))

    in_specs = [pl.BlockSpec((array.shape[0], tile), lambda t, ids, offs: (0, t)) for array in flat]
    in_specs += [block_spec(m) for m in range(n_blocks)]
    operands = flat + [projections] * n_blocks
    aliases = {}
    if before is not None:
        in_specs.append(pl.BlockSpec(memory_space=pl.ANY))
        operands.append(before)
        aliases = {2 + len(operands) - 1: 0}
    if count == 1:
        out_spec = pl.BlockSpec((1, *shape[1:]), lambda t, ids, offs: (ids[0], 0, 0))
    else:
        out_spec = pl.BlockSpec(shape, lambda t, ids, offs: (0, 0, 0))
    return pl.pallas_call(
        body,
        out_shape=jax.ShapeDtypeStruct(shape, jnp.float32),
        grid_spec=pltpu.PrefetchScalarGridSpec(
            num_scalar_prefetch=2,
            grid=(pixels // tile,),
            in_specs=in_specs,
            out_specs=out_spec,
            scratch_shapes=[pltpu.VMEM((count, rows, WIDE), jnp.float32)],
        ),
        input_output_aliases=aliases,
        compiler_params=pltpu.CompilerParams(
            dimension_semantics=("arbitrary",), vmem_limit_bytes=SCORE_VMEM
        ),
        cost_estimate=pl.CostEstimate(
            flops=2 * count * rows * WIDE * pixels,
            bytes_accessed=count * (rows + WIDE) * pixels * 2 + count * rows * WIDE * 4,
            transcendentals=0,
        ),
        name="scores",
    )(group_ids, offsets, *[in_hbm(array) for array in operands])


def softmax_body(used_ref, total_ref, scale_ref, weight_ref, evidence_ref):
    n = total_ref.shape[0]
    scale = scale_ref[...]
    peak = jnp.full(scale.shape, -jnp.inf, jnp.float32)

    def logits(o, j):
        value = total_ref[o, :, j * BLOCK : (j + 1) * BLOCK] * scale
        live = used_ref[o * CAP + j] > 0
        return jnp.where(live, value, jnp.float32(-1e30)), live

    for o in range(n):
        for j in range(CAP):
            peak = jnp.maximum(peak, jnp.max(logits(o, j)[0], axis=1, keepdims=True))
    total = jnp.zeros(scale.shape, jnp.float32)
    for o in range(n):
        for j in range(CAP):
            value, live = logits(o, j)
            raised = jnp.where(live, jnp.exp(value - peak), jnp.float32(0.0))
            total_ref[o, :, j * BLOCK : (j + 1) * BLOCK] = raised
            total = total + jnp.sum(raised, axis=1, keepdims=True)
    for o in range(n):
        weight_ref[o] = (total_ref[o] / total).astype(jnp.bfloat16)
    marginal = jnp.broadcast_to(peak + jnp.log(total), (total.shape[0], BLOCK))
    evidence_ref[...] = marginal.T[:1]


def softmax(totals, scale, used):
    n, share, _ = totals.shape

    def body(used_ref, total_in, scale_ref, weight_ref, evidence_ref, work):
        work[...] = total_in[...]
        softmax_body(used_ref, work, scale_ref, weight_ref, evidence_ref)

    return pl.pallas_call(
        body,
        out_shape=(
            jax.ShapeDtypeStruct((n, share, WIDE), jnp.bfloat16),
            jax.ShapeDtypeStruct((1, share), jnp.float32),
        ),
        in_specs=[
            pl.BlockSpec(memory_space=pltpu.SMEM),
            pl.BlockSpec(memory_space=pltpu.VMEM),
            pl.BlockSpec(memory_space=pltpu.VMEM),
        ],
        out_specs=(
            pl.BlockSpec(memory_space=pltpu.VMEM),
            pl.BlockSpec(memory_space=pltpu.VMEM),
        ),
        scratch_shapes=[pltpu.VMEM((n, share, WIDE), jnp.float32)],
        compiler_params=pltpu.CompilerParams(vmem_limit_bytes=16 << 20),
        cost_estimate=pl.CostEstimate(
            flops=6 * n * share * WIDE,
            bytes_accessed=6 * n * share * WIDE,
            transcendentals=n * share * WIDE,
        ),
        name="softmax",
    )(used, totals, scale)


def sums_kernel(images_of, weights, group_ids, offsets, owned_rows, pixels, n):
    tile = 512 if pixels % 512 == 0 else pixels
    flat_images, place = [], []
    for r, entries in enumerate(images_of):
        place.append([])
        for array in entries:
            place[r].append(len(flat_images))
            flat_images.append(array)
    n_images, n_weights = len(flat_images), len(weights)
    depth = sum(array.shape[1] for array in weights)

    def body(ids_ref, offs_ref, *refs):
        image_refs = refs[:n_images]
        weight_refs = refs[n_images : n_images + n_weights]
        out_ref, rows_ref, cols_ref = refs[n_images + n_weights :]

        @pl.when(pl.program_id(0) == 0)
        def _():
            first = 0
            for ref in weight_refs:
                rows_ref[:, first : first + ref.shape[1], :] = ref[...]
                first += ref.shape[1]
            for g in range(n):
                cols_ref[g] = rows_ref[g].T

        out_ref[...] = jnp.zeros_like(out_ref)
        for r in range(n):
            g = ids_ref[r]
            rows = jnp.concatenate([image_refs[i][...] for i in place[r]], axis=0)
            sums = jnp.dot(cols_ref[g], rows, preferred_element_type=jnp.float32)
            sums = sums.astype(jnp.bfloat16).astype(jnp.float32)
            for j in range(CAP):
                at = pl.ds(pl.multiple_of(offs_ref[g * CAP + j] * BLOCK, BLOCK), BLOCK)
                out_ref[at, :] += sums[j * BLOCK : (j + 1) * BLOCK]

    return pl.pallas_call(
        body,
        out_shape=jax.ShapeDtypeStruct((owned_rows, pixels), jnp.float32),
        grid_spec=pltpu.PrefetchScalarGridSpec(
            num_scalar_prefetch=2,
            grid=(pixels // tile,),
            in_specs=[
                pl.BlockSpec((array.shape[0], tile), lambda t, ids, offs: (0, t))
                for array in flat_images
            ]
            + [pl.BlockSpec(array.shape, lambda t, ids, offs: (0, 0, 0)) for array in weights],
            out_specs=pl.BlockSpec((owned_rows, tile), lambda t, ids, offs: (0, t)),
            scratch_shapes=[
                pltpu.VMEM((n, depth, WIDE), jnp.bfloat16),
                pltpu.VMEM((n, WIDE, depth), jnp.bfloat16),
            ],
        ),
        compiler_params=pltpu.CompilerParams(
            dimension_semantics=("arbitrary",), vmem_limit_bytes=SUMS_VMEM
        ),
        cost_estimate=pl.CostEstimate(
            flops=2 * n * depth * WIDE * pixels,
            bytes_accessed=n * depth * (pixels + WIDE) * 2 + owned_rows * pixels * 4,
            transcendentals=0,
        ),
        name="sums",
    )(group_ids, offsets, *[in_hbm(array) for array in flat_images], *weights)


def on_device(images, inverse_noise_scale, projections, group_search_blocks, search_list_count):
    group_rows, pixels = images.shape
    n = lax.axis_size("img")
    n_pix = lax.axis_size("pix")
    n_x = n_pix // CORES
    owned = projections.shape[0] // BLOCK
    me = lax.axis_index("img")
    pix = lax.axis_index("pix")
    my_x, my_core = pix // CORES, pix % CORES
    share_rows = group_rows // n_pix

    ring = ring_order(n)
    to_right = [(ring[k], ring[(k + 1) % n]) for k in range(n)]
    to_left = [(b, a) for a, b in to_right]
    ring_ids = jnp.array(ring, jnp.int32)
    pos_table = [0] * n
    for k, index in enumerate(ring):
        pos_table[index] = k
    ring_pos = jnp.array(pos_table, jnp.int32)
    my_pos = ring_pos[me]
    shifts = [0]
    for s in range(1, n // 2):
        shifts += [-s, s]
    shifts.append(n // 2)
    group_ids = ring_ids[(my_pos + jnp.array(shifts, jnp.int32)) % n]

    scale_mine = lax.dynamic_slice_in_dim(inverse_noise_scale, pix * share_rows, share_rows)

    note = jnp.concatenate(
        [group_search_blocks[0], search_list_count, jnp.zeros((2 * MAXL - MAXL - 1,), jnp.int32)]
    )
    notes = lax.all_to_all(jnp.broadcast_to(note, (n, 2 * MAXL)), "img", 0, 0, tiled=True)
    positions = jnp.arange(MAXL, dtype=jnp.int32)
    slots = jnp.arange(CAP, dtype=jnp.int32)

    def slot_table(notes):
        lists, counts = notes[:, :MAXL], notes[:, MAXL]
        hit = (positions[None, :] < counts[:, None]) & (lists // owned == me)
        earlier = positions[None, :] < positions[:, None]
        rank = jnp.sum((hit[:, None, :] & earlier[None]).astype(jnp.int32), axis=2)
        pick = hit[:, None, :] & (rank[:, None, :] == slots[None, :, None])
        slot_offset = jnp.sum(jnp.where(pick, (lists % owned)[:, None, :], 0), axis=2)
        return slot_offset.reshape(-1), slot_offset[group_ids].reshape(-1)

    own_live = positions < search_list_count[0]
    own_owner = group_search_blocks[0] // owned
    per_owner = jnp.sum(
        (own_live[None, :] & (own_owner[None, :] == jnp.arange(n, dtype=jnp.int32)[:, None])).astype(
            jnp.int32
        ),
        axis=1,
    )
    used = (slots[None, :] < per_owner[:, None]).astype(jnp.int32).reshape(-1)

    core_swap = [(p, p ^ 1) for p in range(n_pix)]

    def x_shift(k):
        return [
            (x * CORES + core, ((x + k) % n_x) * CORES + core)
            for x in range(n_x)
            for core in range(CORES)
        ]

    unit = share_rows // sum(CHUNK_PARTS)
    shares = [unit * part for part in CHUNK_PARTS]
    starts = [sum(shares[:c]) for c in range(len(shares))]
    far_step = n // 2

    def packet(c, a):
        rows = []
        for b in range(n_x):
            q = ((my_x + b) % n_x) * CORES + (my_core ^ a)
            rows.append(
                lax.dynamic_slice_in_dim(images, q * share_rows + starts[c], shares[c], axis=0)
            )
        return jnp.concatenate(rows, axis=0)

    messages = [
        (c, a, s) for c in range(len(shares)) for s in range(1, far_step + 1) for a in (1, 0)
    ]
    pieces = {(c, a): {} for c in range(len(shares)) for a in (0, 1)}
    scores, score_tick = {}, {}

    def score(c, a, places):
        rows = shares[c] * n_x
        piece_offset = offsets[1]
        scores[c, a] = score_pieces(
            [pieces[c, a][r] for r in places],
            group_ids[places[0] : places[-1] + 1],
            piece_offset[places[0] * CAP : (places[-1] + 1) * CAP],
            projections,
            scores.get((c, a)),
            (n, rows, WIDE),
        )

    weights_of, evidence = {}, {}

    def finish(c):
        share = shares[c]
        (got,) = yield [lax.ppermute(scores[c, 1], "pix", core_swap)], 1
        whole = (scores[c, 0] + got).reshape(n, n_x, share, WIDE)
        parts = [whole[:, 0]] + [
            lax.ppermute(whole[:, b], "pix", x_shift(b)) for b in range(1, n_x)
        ]
        parts = yield parts, 1
        total = parts[0]
        for part in parts[1:]:
            total = total + part
        (home,) = yield [lax.all_to_all(total, "img", 0, 0, tiled=True)], 2
        scale = lax.slice_in_dim(scale_mine, starts[c], starts[c] + share).reshape(share, 1)
        weights, marginal = softmax(home, scale, used)
        evidence[c] = marginal.reshape(share)
        (back,) = yield [lax.all_to_all(weights, "img", 0, 0, tiled=True)], 2
        same = yield [back] + [lax.ppermute(back, "pix", x_shift(-b)) for b in range(1, n_x)], 1
        other = yield [lax.ppermute(array, "pix", core_swap) for array in same], 1
        weights_of[c] = [*same, *other]

    arrived = {}
    due = {LIST_TICK: [(None, [notes])]}
    offsets = None
    running = {}

    def advance(c, sent):
        try:
            values, lag = running[c].send(sent)
            due.setdefault(tick + lag, []).append((c, list(values)))
        except StopIteration:
            pass

    tick = 0
    while tick < len(messages) + 2 or any(t >= tick for t in due):
        flying = tick < len(messages)
        ring = []
        if tick >= 2 and tick - 2 in arrived:
            ring += list(arrived[tick - 2])
        n_arrived = len(ring)
        fresh = flying and messages[tick][2] == 1
        if fresh:
            ring.append(packet(*messages[tick][:2]))
        waiting = due.pop(tick, [])
        scored = [key for key in scores if score_tick.get(key) == tick] if tick else []
        bundle = ring + [scores[key] for key in scored] + [v for _, vs in waiting for v in vs]
        if tick >= 2 and len(bundle) > 1:
            bundle = list(lax.optimization_barrier(tuple(bundle)))
        ring, rest = bundle[: len(ring)], bundle[len(ring) :]
        for key in scored:
            scores[key] = rest.pop(0)
        if n_arrived:
            arrived[tick - 2] = ring[:2]
            c, a, s = messages[tick - 2]
            if s == far_step:
                pieces[c, a][n - 1] = ring[:2]
            else:
                pieces[c, a][2 * s - 1], pieces[c, a][2 * s] = [ring[0]], [ring[1]]
        if flying:
            c, a, s = messages[tick]
            if fresh:
                pieces[c, a][0] = [ring[-1]]
                left = right = ring[-1]
            else:
                left, right = pieces[c, a][2 * s - 3][0], pieces[c, a][2 * s - 2][0]
            if s == far_step:
                middle = left.shape[0] // 2
                left, right = left[:middle], right[middle:]
            arrived[tick] = (
                lax.ppermute(left, "img", to_right),
                lax.ppermute(right, "img", to_left),
            )
        if n_arrived:
            c, a, s = messages[tick - 2]
            if s >= far_step - 1:
                score(c, a, [n - 1] if s == far_step else list(range(n - 1)))
                score_tick[c, a] = tick + 1
        for c, values in waiting:
            sent, rest = rest[: len(values)], rest[len(values) :]
            if c is None:
                offsets = slot_table(sent[0])
            else:
                advance(c, sent)
        for c in range(len(shares)):
            if c not in running and messages.index((c, 1, far_step)) + 3 == tick:
                running[c] = finish(c)
                advance(c, None)
        tick += 1

    images_of = [
        [array for c in range(len(shares)) for a in (0, 1) for array in pieces[c, a][r]]
        for r in range(n)
    ]
    weights = [array for c in range(len(shares)) for array in weights_of[c]]
    sums = sums_kernel(images_of, weights, group_ids, offsets[0], owned * BLOCK, pixels, n)
    return sums, jnp.concatenate([evidence[c] for c in range(len(shares))])


def solution(mesh):
    placed = (P("img", "pix"), P("img"), P("img", "pix"), P("img", None), P("img"))
    return jax.shard_map(
        on_device,
        mesh=mesh,
        in_specs=placed,
        out_specs=(P("img", "pix"), P(("img", "pix"))),
        check_vma=False,
    )
```

```python
import jax
import jax.numpy as jnp
from jax import lax
from jax.experimental import pallas as pl
from jax.experimental.pallas import tpu as pltpu
from jax.sharding import PartitionSpec as P


BLOCK = 128
CAP = 2
MAXL = 16
WIDE = CAP * BLOCK
CORES = 2
CHUNK_PARTS = (2, 1)
SCORE_VMEM = 60 << 20
SUMS_VMEM = 28 << 20
LIGHT = pl.CostEstimate(flops=1, bytes_accessed=1, transcendentals=0)


def ring_order(n):
    rows = 4 if n % 4 == 0 and n >= 8 else 1
    cols = n // rows
    if rows == 1 or cols == 1:
        return list(range(n))
    walk = []
    for row in range(rows):
        across = range(1, cols) if row % 2 == 0 else range(cols - 1, 0, -1)
        walk += [row * cols + col for col in across]
    return walk + [row * cols for row in range(rows - 1, -1, -1)]


def in_hbm(array):
    return pltpu.with_memory_space_constraint(array, pltpu.HBM)


def score_pieces(packs, group_ids, offsets, projections, before, n):
    count = len(packs[0])
    pixels = projections.shape[1]
    tile = 1024 if pixels % 1024 == 0 else pixels
    heights = [sum(array.shape[0] for array in pack[0]) for pack in packs]
    owned = projections.shape[0] // BLOCK
    whole = count * CAP > owned
    flat = [array for pack in packs for piece in pack for array in piece]
    place, at = [], 0
    for pack in packs:
        place.append([])
        for piece in pack:
            place[-1].append(list(range(at, at + len(piece))))
            at += len(piece)
    n_flat, n_blocks, n_packs = len(flat), 1 if whole else count * CAP, len(packs)
    n_in = n_flat + n_blocks + (n_packs if before else 0)

    def body(ids_ref, offs_ref, *refs):
        row_refs, block_refs = refs[:n_flat], refs[n_flat : n_flat + n_blocks]
        out_refs = refs[n_in : n_in + n_packs]
        acc_ref, sems = refs[n_in + n_packs :]
        step, last = pl.program_id(0), pl.num_programs(0) - 1

        @pl.when(step == 0)
        def _():
            acc_ref[...] = jnp.zeros_like(acc_ref)

        for k in range(count):
            left = [row_refs[i][...] for p in range(n_packs) for i in place[p][k]]
            right = []
            for j in range(CAP):
                if whole:
                    first = pl.multiple_of(offs_ref[k * CAP + j] * BLOCK, BLOCK)
                    right.append(block_refs[0][pl.ds(first, BLOCK), :])
                else:
                    right.append(block_refs[k * CAP + j][...])
            acc_ref[k] += lax.dot_general(
                jnp.concatenate(left, axis=0),
                jnp.concatenate(right, axis=0),
                (((1,), (1,)), ((), ())),
                preferred_element_type=jnp.float32,
            )

        @pl.when(step == last)
        def _():
            copies = []
            for k in range(count):
                first = 0
                for p in range(n_packs):
                    copies.append(
                        pltpu.make_async_copy(
                            acc_ref.at[k, pl.ds(first, heights[p])],
                            out_refs[p].at[ids_ref[k]],
                            sems.at[k * n_packs + p],
                        )
                    )
                    first += heights[p]
            for copy in copies:
                copy.start()
            for copy in copies:
                copy.wait()

    in_specs = [pl.BlockSpec((array.shape[0], tile), lambda t, ids, offs: (0, t)) for array in flat]
    if whole:
        in_specs.append(pl.BlockSpec((projections.shape[0], tile), lambda t, ids, offs: (0, t)))
    else:
        in_specs += [
            pl.BlockSpec((BLOCK, tile), lambda t, ids, offs, m=m: (offs[m], t))
            for m in range(n_blocks)
        ]
    operands = [in_hbm(array) for array in [*flat, *[projections] * n_blocks]]
    aliases = {}
    for p, array in enumerate(before or ()):
        in_specs.append(pl.BlockSpec(memory_space=pl.ANY))
        operands.append(in_hbm(array))
        aliases[2 + len(operands) - 1] = p
    rows = sum(heights)
    return pl.pallas_call(
        body,
        out_shape=[jax.ShapeDtypeStruct((n, h, WIDE), jnp.float32) for h in heights],
        grid_spec=pltpu.PrefetchScalarGridSpec(
            num_scalar_prefetch=2,
            grid=(pixels // tile,),
            in_specs=in_specs,
            out_specs=[pl.BlockSpec(memory_space=pltpu.HBM) for _ in heights],
            scratch_shapes=[
                pltpu.VMEM((count, rows, WIDE), jnp.float32),
                pltpu.SemaphoreType.DMA((count * n_packs,)),
            ],
        ),
        input_output_aliases=aliases,
        compiler_params=pltpu.CompilerParams(
            dimension_semantics=("arbitrary",), vmem_limit_bytes=SCORE_VMEM
        ),
        cost_estimate=LIGHT,
        name="scores",
    )(group_ids, offsets, *operands)


def softmax_body(used_ref, total_ref, scale_ref, weight_ref, evidence_ref):
    n = total_ref.shape[0]
    scale = scale_ref[...]
    peak = jnp.full(scale.shape, -jnp.inf, jnp.float32)

    def logits(o, j):
        value = total_ref[o, :, j * BLOCK : (j + 1) * BLOCK] * scale
        live = used_ref[o * CAP + j] > 0
        return jnp.where(live, value, jnp.float32(-1e30)), live

    for o in range(n):
        for j in range(CAP):
            peak = jnp.maximum(peak, jnp.max(logits(o, j)[0], axis=1, keepdims=True))
    total = jnp.zeros(scale.shape, jnp.float32)
    for o in range(n):
        for j in range(CAP):
            value, live = logits(o, j)
            raised = jnp.where(live, jnp.exp(value - peak), jnp.float32(0.0))
            total_ref[o, :, j * BLOCK : (j + 1) * BLOCK] = raised
            total = total + jnp.sum(raised, axis=1, keepdims=True)
    for o in range(n):
        weight_ref[o] = (total_ref[o] / total).astype(jnp.bfloat16)
    marginal = jnp.broadcast_to(peak + jnp.log(total), (total.shape[0], BLOCK))
    evidence_ref[...] = marginal.T[:1]


def softmax(totals, scale, used):
    n, share, _ = totals.shape

    def body(used_ref, total_in, scale_ref, weight_ref, evidence_ref, work):
        work[...] = total_in[...]
        softmax_body(used_ref, work, scale_ref, weight_ref, evidence_ref)

    return pl.pallas_call(
        body,
        out_shape=(
            jax.ShapeDtypeStruct((n, share, WIDE), jnp.bfloat16),
            jax.ShapeDtypeStruct((1, share), jnp.float32),
        ),
        in_specs=[
            pl.BlockSpec(memory_space=pltpu.SMEM),
            pl.BlockSpec(memory_space=pltpu.VMEM),
            pl.BlockSpec(memory_space=pltpu.VMEM),
        ],
        out_specs=(
            pl.BlockSpec(memory_space=pltpu.VMEM),
            pl.BlockSpec(memory_space=pltpu.VMEM),
        ),
        scratch_shapes=[pltpu.VMEM((n, share, WIDE), jnp.float32)],
        compiler_params=pltpu.CompilerParams(vmem_limit_bytes=16 << 20),
        cost_estimate=LIGHT,
        name="softmax",
    )(used, totals, scale)


def make_sums(images_of, weights, group_ids, offsets, owned_rows, pixels, n):
    tile = 512 if pixels % 512 == 0 else pixels
    flat, place = [], []
    for entries in images_of:
        place.append(list(range(len(flat), len(flat) + len(entries))))
        flat += entries
    n_images, n_weights = len(flat), len(weights)
    depth = sum(array.shape[1] for array in weights)

    def body(ids_ref, offs_ref, *refs):
        image_refs = refs[:n_images]
        weight_refs = refs[n_images : n_images + n_weights]
        out_ref, rows_ref, cols_ref = refs[n_images + n_weights :]

        @pl.when(pl.program_id(0) == 0)
        def _():
            first = 0
            for ref in weight_refs:
                rows_ref[:, first : first + ref.shape[1], :] = ref[...]
                first += ref.shape[1]
            for g in range(n):
                cols_ref[g] = rows_ref[g].T

        out_ref[...] = jnp.zeros_like(out_ref)
        for r in range(n):
            g = ids_ref[r]
            rows = jnp.concatenate([image_refs[i][...] for i in place[r]], axis=0)
            sums = jnp.dot(cols_ref[g], rows, preferred_element_type=jnp.float32)
            sums = sums.astype(jnp.bfloat16).astype(jnp.float32)
            for j in range(CAP):
                at = pl.ds(pl.multiple_of(offs_ref[g * CAP + j] * BLOCK, BLOCK), BLOCK)
                out_ref[at, :] += sums[j * BLOCK : (j + 1) * BLOCK]

    return pl.pallas_call(
        body,
        out_shape=jax.ShapeDtypeStruct((owned_rows, pixels), jnp.float32),
        grid_spec=pltpu.PrefetchScalarGridSpec(
            num_scalar_prefetch=2,
            grid=(pixels // tile,),
            in_specs=[
                pl.BlockSpec((array.shape[0], tile), lambda t, ids, offs: (0, t)) for array in flat
            ]
            + [pl.BlockSpec(array.shape, lambda t, ids, offs: (0, 0, 0)) for array in weights],
            out_specs=pl.BlockSpec((owned_rows, tile), lambda t, ids, offs: (0, t)),
            scratch_shapes=[
                pltpu.VMEM((n, depth, WIDE), jnp.bfloat16),
                pltpu.VMEM((n, WIDE, depth), jnp.bfloat16),
            ],
        ),
        compiler_params=pltpu.CompilerParams(
            dimension_semantics=("arbitrary",), vmem_limit_bytes=SUMS_VMEM
        ),
        cost_estimate=LIGHT,
        name="sums",
    )(group_ids, offsets, *[in_hbm(array) for array in flat], *weights)


def on_device(images, inverse_noise_scale, projections, group_search_blocks, search_list_count):
    group_rows, pixels = images.shape
    n = lax.axis_size("img")
    n_pix = lax.axis_size("pix")
    n_x = n_pix // CORES
    owned = projections.shape[0] // BLOCK
    me = lax.axis_index("img")
    pix = lax.axis_index("pix")
    my_x, my_core = pix // CORES, pix % CORES
    share_rows = group_rows // n_pix

    ring = ring_order(n)
    to_right = [(ring[k], ring[(k + 1) % n]) for k in range(n)]
    to_left = [(b, a) for a, b in to_right]
    ring_ids = jnp.array(ring, jnp.int32)
    pos_table = [0] * n
    for k, index in enumerate(ring):
        pos_table[index] = k
    ring_pos = jnp.array(pos_table, jnp.int32)
    my_pos = ring_pos[me]
    shifts = [0]
    for s in range(1, n // 2):
        shifts += [-s, s]
    shifts.append(n // 2)
    group_ids = ring_ids[(my_pos + jnp.array(shifts, jnp.int32)) % n]

    scale_mine = lax.dynamic_slice_in_dim(inverse_noise_scale, pix * share_rows, share_rows)

    note = jnp.concatenate(
        [group_search_blocks[0], search_list_count, jnp.zeros((2 * MAXL - MAXL - 1,), jnp.int32)]
    )
    notes = lax.all_to_all(jnp.broadcast_to(note, (n, 2 * MAXL)), "img", 0, 0, tiled=True)
    positions = jnp.arange(MAXL, dtype=jnp.int32)
    slots = jnp.arange(CAP, dtype=jnp.int32)

    def slot_table(notes):
        lists, counts = notes[:, :MAXL], notes[:, MAXL]
        hit = (positions[None, :] < counts[:, None]) & (lists // owned == me)
        earlier = positions[None, :] < positions[:, None]
        rank = jnp.sum((hit[:, None, :] & earlier[None]).astype(jnp.int32), axis=2)
        pick = hit[:, None, :] & (rank[:, None, :] == slots[None, :, None])
        slot_offset = jnp.sum(jnp.where(pick, (lists % owned)[:, None, :], 0), axis=2)
        return slot_offset.reshape(-1), slot_offset[group_ids].reshape(-1)

    own_live = positions < search_list_count[0]
    own_owner = group_search_blocks[0] // owned
    per_owner = jnp.sum(
        (own_live[None, :] & (own_owner[None, :] == jnp.arange(n, dtype=jnp.int32)[:, None])).astype(
            jnp.int32
        ),
        axis=1,
    )
    used = (slots[None, :] < per_owner[:, None]).astype(jnp.int32).reshape(-1)

    core_swap = [(p, p ^ 1) for p in range(n_pix)]

    def x_shift(k):
        return [
            (x * CORES + core, ((x + k) % n_x) * CORES + core)
            for x in range(n_x)
            for core in range(CORES)
        ]

    unit = share_rows // sum(CHUNK_PARTS)
    shares = [unit * part for part in CHUNK_PARTS]
    starts = [sum(shares[:c]) for c in range(len(shares))]
    far_step = n // 2

    def packet(c, a):
        rows = []
        for b in range(n_x):
            q = ((my_x + b) % n_x) * CORES + (my_core ^ a)
            rows.append(
                lax.dynamic_slice_in_dim(images, q * share_rows + starts[c], shares[c], axis=0)
            )
        return jnp.concatenate(rows, axis=0)

    chunks = range(len(shares))
    pieces = {(c, a): {} for c in chunks for a in (0, 1)}
    offsets, piece_offsets = slot_table(notes)

    def send(array, way):
        return lax.ppermute(array, "img", to_right if way == "R" else to_left)

    def score(c, places, before):
        return score_pieces(
            [[pieces[c, a][r] for r in places] for a in (0, 1)],
            group_ids[places[0] : places[-1] + 1],
            piece_offsets[places[0] * CAP : (places[-1] + 1) * CAP],
            projections,
            before,
            n,
        )

    images_of = [[] for _ in range(n)]
    weights_of, evidence = [], []
    for c in chunks:
        share = shares[c]
        for a in (1, 0):
            left = right = packet(c, a)
            pieces[c, a][0] = [left]
            for s in range(1, far_step):
                left, right = send(left, "R"), send(right, "L")
                pieces[c, a][2 * s - 1], pieces[c, a][2 * s] = [left], [right]
            far = send(left, "R") if a else send(right, "L")
            pieces[c, a][n - 1] = [far]
        for r in range(n):
            images_of[r] += pieces[c, 0][r] + pieces[c, 1][r]

        scores = score(c, list(range(n - 3)), None)
        scores = score(c, [n - 3, n - 2], scores)
        keep, give = score(c, [n - 1], scores)
        got = lax.ppermute(give, "pix", core_swap)
        whole = (keep + got).reshape(n, n_x, share, WIDE)
        total = whole[:, 0]
        for b in range(1, n_x):
            total = total + lax.ppermute(whole[:, b], "pix", x_shift(b))
        home = lax.all_to_all(total, "img", 0, 0, tiled=True)
        scale = lax.slice_in_dim(scale_mine, starts[c], starts[c] + share).reshape(share, 1)
        weights, marginal = softmax(home, scale, used)
        evidence.append(marginal.reshape(share))
        back = lax.all_to_all(weights, "img", 0, 0, tiled=True)
        same = [back] + [lax.ppermute(back, "pix", x_shift(-b)) for b in range(1, n_x)]
        other = [lax.ppermute(array, "pix", core_swap) for array in same]
        weights_of += [*same, *other]

    sums = make_sums(images_of, weights_of, group_ids, offsets, owned * BLOCK, pixels, n)
    return sums, jnp.concatenate(evidence)


def solution(mesh):
    placed = (P("img", "pix"), P("img"), P("img", "pix"), P("img", None), P("img"))

    return jax.shard_map(
        on_device,
        mesh=mesh,
        in_specs=placed,
        out_specs=(P("img", "pix"), P(("img", "pix"))),
        check_vma=False,
    )
```
